32 devices in a mesh: grp: 2 (over y), ft: 4 (over z), bl: 4 (over x, core).
Axes of the slice: x: 2, y: 2, z: 4, core: 2. Of those that a mesh axis runs over, the one named last changes fastest.
Arguments:
- voltages: bfloat16 [2, 16384, 1024], P(None, ('grp', 'ft'), 'bl'), parts along dimension 1, may hold values from -11 to 11
- coefs: float32 [8, 2048], replicated, may hold values from -2 to 2
- block_ids: int32 [4], replicated, may hold values from 0 to 3, each once
- tile_owner: int32 [20], P('grp'), parts along dimension 0, may hold values from 0 to 3, as said below
Outputs:
- vis: float32 [2, 64, 20, 256, 256], P(None, ('grp', 'ft'), 'bl'), parts along dimension 1
The draws below stay inside these ranges and needn't reach their ends.
There are 2 independent parts, one for each index of `grp`. The reference program is written for one: setup_inputs(seed, part) draws one part's arguments, and reference() takes and returns one part's arrays. A program takes and returns all parts, laid end to end along the dimension named above; an argument that names none is the same for every part. Nothing has to cross between parts.
Inputs may be any that keep to these rules, and one draw needn't show every extreme that they name: tile_owner[t] is the index along bl of the device that owns tile t; one owner holds exactly 5 tiles, the others share the remaining tiles as evenly as counts allow.
All inputs are finite; a program needn't handle non-finite values.
Results may differ from the reference program's by a relative error of at most 0.00099.
Values may be sent and summed in bfloat16 or wider, within the bound.
A program may use at most 128 MiB of HBM per device.

```python
import math
import jax
import jax.numpy as jnp
import numpy as np
from jax import lax

NIN = 1024
NCH = 2048
TAPS = 8
AVG = 64
SPECTRA = 4
TIME = 8192
NB = 4
BLK = 256
NTILES = 10
MAXT = 5
COARSE = 32


def draw_voltages(key, part):
    key_signal, key_delay, key_gain, key_noise = jax.random.split(key, 4)
    delay_span = 16
    signal = jnp.clip(jax.random.normal(key_signal, (2, TIME + delay_span), jnp.float32), -5.0, 5.0)
    delays = jax.random.randint(key_delay, (NIN,), 0, delay_span)
    gain_of = jax.random.uniform(key_gain, (NIN,), jnp.float32, 0.3, 1.0)
    noise_part = jnp.clip(jax.random.normal(key_noise, (2, TIME, NIN), jnp.float32), -5.0, 5.0)
    source_pos = jnp.arange(TIME, dtype=jnp.int32)[:, None] + (delay_span - delays)[None, :]
    delayed = signal[:, source_pos]
    return (gain_of[None, None, :] * delayed + noise_part).astype(jnp.bfloat16)


def draw_tile_owner(key, part):
    key_heavy, key_order, key_offset = jax.random.split(key, 3)
    heavy_owner = jax.random.randint(key_heavy, (), 0, NB)
    tile_order = jax.random.permutation(key_order, NTILES)
    position = jnp.argsort(tile_order)
    spread_offset = jax.random.randint(key_offset, (), 0, NB - 1)
    other_owner = (heavy_owner + 1 + (position - MAXT + spread_offset) % (NB - 1)) % NB
    return jnp.where(position < MAXT, heavy_owner, other_owner).astype(jnp.int32)


def gaussian(own_key, dims, deviation, most, held_as=jnp.bfloat16):
    values = jax.random.normal(own_key, dims, jnp.float32) * deviation
    return jnp.minimum(jnp.maximum(values, -most), most).astype(held_as)


def setup_inputs(seed: int = 0, part: int = 0) -> dict:
    key_list = jax.random.split(jax.random.key(seed), 5)
    part_keys = jax.random.split(jax.random.fold_in(key_list[4], part), 5)
    voltages = draw_voltages(jax.random.fold_in(jax.random.fold_in(key_list[4], part), 71), part)
    coefs = gaussian(key_list[1], (TAPS, NCH), TAPS ** -0.5, 2.0, jnp.float32)
    block_ids = jax.random.permutation(key_list[2], NB).astype(jnp.int32)
    tile_owner = draw_tile_owner(jax.random.fold_in(jax.random.fold_in(key_list[4], part), 71), part)
    return {"voltages": voltages, "coefs": coefs, "block_ids": block_ids, "tile_owner": tile_owner}


def reference(voltages, coefs, block_ids, tile_owner):
    by_block = voltages.reshape(2, SPECTRA, NCH, NB, BLK).transpose(3, 0, 1, 2, 4)

    def channelize(block_data):
        samples = block_data.astype(jnp.float32)
        padded = jnp.concatenate([jnp.zeros((2, TAPS - 1, NCH, BLK), jnp.float32), samples], axis=1)
        filtered = jnp.zeros((2, SPECTRA, NCH, BLK), jnp.float32)
        for tap_index in range(TAPS):
            filtered = filtered + coefs[tap_index][None, None, :, None] * padded[:, tap_index:tap_index + SPECTRA]
        complex_out = jnp.fft.fft(filtered[0] + 1j * filtered[1], axis=1) * (1.0 / math.sqrt(NCH))
        return jnp.stack([jnp.real(complex_out), jnp.imag(complex_out)]).astype(jnp.bfloat16)
    spectra = lax.map(channelize, by_block)
    spectra_all = spectra.reshape(NB, 2, SPECTRA, COARSE, AVG, BLK)
    labels = jnp.arange(NB, dtype=jnp.int32)
    shard_of = lax.optimization_barrier(jnp.sum(jnp.where(block_ids[None, :] == labels[:, None], labels[None, :], 0), axis=1)).astype(jnp.int32)
    row_table = np.array([first_id for first_id in range(NB) for second_id in range(first_id, NB)], dtype=np.int32)
    col_table = np.array([second_id for first_id in range(NB) for second_id in range(first_id, NB)], dtype=np.int32)
    pair_ids = jnp.stack([jnp.asarray(row_table), jnp.asarray(col_table)], axis=1)

    def correlate(pair_row):
        row_data = spectra_all[shard_of[pair_row[0]]].astype(jnp.float32)
        col_data = spectra_all[shard_of[pair_row[1]]].astype(jnp.float32)
        products = jnp.einsum('pscax,qscay->cpqxy', row_data, col_data, precision=lax.Precision.HIGHEST)
        real_part = products[:, 0, 0] + products[:, 1, 1]
        imag_part = products[:, 1, 0] - products[:, 0, 1]
        return jnp.stack([real_part, imag_part]) * (1.0 / (AVG * SPECTRA))
    tiles = lax.map(correlate, pair_ids)
    tile_pos = jnp.arange(NTILES, dtype=jnp.int32)
    same_owner = tile_owner[None, :] == tile_owner[:, None]
    before_mask = tile_pos[None, :] < tile_pos[:, None]
    slot_rank = lax.optimization_barrier(jnp.sum((same_owner & before_mask).astype(jnp.int32), axis=1)).astype(jnp.int32)
    dest_slot = (tile_owner * MAXT + slot_rank).astype(jnp.int32)
    vis = jnp.zeros((2, COARSE, NB * MAXT, BLK, BLK), jnp.float32)
    return vis.at[:, :, dest_slot].set(tiles.transpose(1, 2, 0, 3, 4))
```

```python
import functools
import math

import jax
import jax.numpy as jnp
import numpy as np
from jax import lax
from jax.experimental import pallas as pl
from jax.experimental.pallas import tpu as pltpu
from jax.sharding import PartitionSpec as P

AVG = 64


def tile_product(row_part, col_part, norm_scale):
    products = jnp.einsum(
        "pscax,qscay->cpqxy", row_part, col_part, preferred_element_type=jnp.float32
    )
    real_part = products[:, 0, 0] + products[:, 1, 1]
    imag_part = products[:, 1, 0] - products[:, 0, 1]
    return jnp.stack([real_part, imag_part]) * norm_scale


def dft_tables(order_len):
    steps_one = jnp.arange(order_len, dtype=jnp.int32)
    phase_grid = steps_one[:, None] * steps_one[None, :] % order_len
    angles = phase_grid.astype(jnp.float32) * (2.0 * math.pi / order_len)
    return (jnp.cos(angles), jnp.sin(angles))


def transform(filtered):
    per_dev = filtered.shape[1]
    chan_count = filtered.shape[2]
    rows_here = filtered.shape[3]
    outer_len = math.isqrt(chan_count)
    while chan_count % outer_len != 0:
        outer_len = outer_len - 1
    inner_len = chan_count // outer_len
    highest = lax.Precision.HIGHEST
    reshaped = filtered.reshape(2, per_dev, outer_len, inner_len, rows_here)
    real_in = reshaped[0]
    imag_in = reshaped[1]
    cos_outer, sin_outer = dft_tables(outer_len)
    section_re = jnp.einsum("snkb,nm->smkb", real_in, cos_outer, precision=highest) + jnp.einsum(
        "snkb,nm->smkb", imag_in, sin_outer, precision=highest
    )
    section_im = jnp.einsum("snkb,nm->smkb", imag_in, cos_outer, precision=highest) - jnp.einsum(
        "snkb,nm->smkb", real_in, sin_outer, precision=highest
    )
    twiddle_grid = (
        jnp.arange(outer_len, dtype=jnp.int32)[:, None]
        * jnp.arange(inner_len, dtype=jnp.int32)[None, :]
        % chan_count
    )
    twiddle_angles = twiddle_grid.astype(jnp.float32) * (2.0 * math.pi / chan_count)
    cos_twiddle = jnp.cos(twiddle_angles)[None, :, :, None]
    sin_twiddle = jnp.sin(twiddle_angles)[None, :, :, None]
    rot_re = section_re * cos_twiddle + section_im * sin_twiddle
    rot_im = section_im * cos_twiddle - section_re * sin_twiddle
    cos_inner, sin_inner = dft_tables(inner_len)
    final_re = jnp.einsum("smkb,kq->sqmb", rot_re, cos_inner, precision=highest) + jnp.einsum(
        "smkb,kq->sqmb", rot_im, sin_inner, precision=highest
    )
    final_im = jnp.einsum("smkb,kq->sqmb", rot_im, cos_inner, precision=highest) - jnp.einsum(
        "smkb,kq->sqmb", rot_re, sin_inner, precision=highest
    )
    stacked = jnp.stack([final_re, final_im]).reshape(2, per_dev, chan_count, rows_here)
    return (stacked * (1.0 / math.sqrt(chan_count))).astype(jnp.bfloat16)


def apply_taps(window, coef_part, taps_count, out_len):
    filtered = jnp.zeros((2, out_len, window.shape[2], window.shape[3]), jnp.float32)
    for tap_index in range(taps_count):
        filtered = filtered + coef_part[tap_index][None, None, :, None] * window[
            :, tap_index : tap_index + out_len
        ].astype(jnp.float32)
    return filtered


def per_device_general(voltages, coefs, block_ids, tile_owner):
    taps_count = coefs.shape[0]
    chan_count = coefs.shape[1]
    rows_here = voltages.shape[2]
    per_dev = voltages.shape[1] // chan_count
    volt_blocks = voltages.reshape(2, per_dev, chan_count, rows_here)
    phase_block = lax.all_to_all(volt_blocks, "ft", split_axis=2, concat_axis=1, tiled=True)
    spectra_count = phase_block.shape[1]
    phase_here = phase_block.shape[2]
    coef_part = lax.dynamic_slice_in_dim(coefs, lax.axis_index("ft") * phase_here, phase_here, 1)
    zero_front = jnp.zeros((2, taps_count - 1, phase_here, rows_here), phase_block.dtype)
    long_window = jnp.concatenate([zero_front, phase_block], axis=1)
    phase_filtered = apply_taps(long_window, coef_part, taps_count, spectra_count)
    filtered = lax.all_to_all(phase_filtered, "ft", split_axis=1, concat_axis=2, tiled=True)
    spectra = transform(filtered)
    turned = lax.all_to_all(spectra, "ft", split_axis=2, concat_axis=1, tiled=True)
    spectra_all = turned.shape[1]
    chan_here = turned.shape[2]
    coarse_here = chan_here // AVG
    coarse_view = turned.reshape(2, spectra_all, coarse_here, AVG, rows_here)
    norm_scale = 1.0 / (AVG * spectra_all)
    block_count = lax.axis_size("bl")
    my_index = lax.axis_index("bl")
    tile_count = block_count * (block_count + 1) // 2
    slot_cap = 2 * tile_count // block_count
    row_table = jnp.asarray(
        np.array(
            [
                first_id
                for first_id in range(block_count)
                for second_id in range(first_id, block_count)
            ],
            dtype=np.int32,
        )
    )
    col_table = jnp.asarray(
        np.array(
            [
                second_id
                for first_id in range(block_count)
                for second_id in range(first_id, block_count)
            ],
            dtype=np.int32,
        )
    )
    tile_pos = jnp.arange(tile_count, dtype=jnp.int32)
    same_owner = tile_owner[None, :] == tile_owner[:, None]
    before_mask = tile_pos[None, :] < tile_pos[:, None]
    slot_rank = jnp.sum((same_owner & before_mask).astype(jnp.int32), axis=1)
    labels = jnp.arange(block_count, dtype=jnp.int32)
    shard_of = jnp.sum(jnp.where(block_ids[None, :] == labels[:, None], labels[None, :], 0), axis=1)
    gathered = lax.all_gather(coarse_view[None], "bl", axis=0, tiled=True)
    mine_mask = tile_owner == my_index
    own_count = jnp.sum(mine_mask.astype(jnp.int32))
    slot_steps = jnp.arange(slot_cap, dtype=jnp.int32)
    slot_tile = jnp.sum(
        jnp.where(
            mine_mask[None, :] & (slot_rank[None, :] == slot_steps[:, None]), tile_pos[None, :], 0
        ),
        axis=1,
    )

    def one_tile(slot_pos, result_tiles):
        tile_id = slot_tile[slot_pos]
        row_block = gathered[shard_of[row_table[tile_id]]]
        col_block = gathered[shard_of[col_table[tile_id]]]
        tile = tile_product(row_block, col_block, norm_scale)
        return lax.dynamic_update_slice(result_tiles, tile[:, :, None], (0, 0, slot_pos, 0, 0))

    empty_tiles = jnp.zeros((2, coarse_here, slot_cap, rows_here, rows_here), jnp.float32)
    return lax.fori_loop(0, own_count, one_tile, empty_tiles)


LANES = 128
RADIX = 16
WINDOW = 2


def split_halves(values):
    high = values.astype(jnp.bfloat16)
    low = (values - high.astype(jnp.float32)).astype(jnp.bfloat16)
    return high, low


def dft_constants(chan_count):
    rows = chan_count // RADIX
    m_grid = np.arange(rows, dtype=np.int64)[None, :, None]
    n_grid = RADIX * np.arange(rows, dtype=np.int64)[None, None, :] + np.arange(RADIX)[:, None, None]
    angles = (m_grid * n_grid % chan_count) * (2.0 * np.pi / chan_count)
    scale = 1.0 / math.sqrt(chan_count)
    parts = []
    for table in (np.cos(angles) * scale, np.sin(angles) * scale):
        high = table.astype(jnp.bfloat16)
        parts.append(high)
        parts.append((table - high.astype(np.float64)).astype(jnp.bfloat16))
    return np.stack([parts[0], parts[2], parts[1], parts[3]], axis=1)


def turn_values(value, step, count):
    re, im = value
    step = step % count
    if step == 0:
        return value
    if 4 * step == count:
        return im, -re
    if 2 * step == count:
        return -re, -im
    if 8 * step == count:
        half = np.float32(math.sqrt(0.5))
        return (re + im) * half, (im - re) * half
    if 8 * step == 3 * count:
        half = np.float32(math.sqrt(0.5))
        return (im - re) * half, -(re + im) * half
    angle = 2.0 * math.pi * step / count
    cos_v, sin_v = np.float32(math.cos(angle)), np.float32(math.sin(angle))
    return re * cos_v + im * sin_v, im * cos_v - re * sin_v


def small_fft(values):
    count = len(values)
    if count == 1:
        return values
    even = small_fft(values[0::2])
    odd = small_fft(values[1::2])
    first, second = [], []
    for pos in range(count // 2):
        turned = turn_values(odd[pos], pos, count)
        first.append((even[pos][0] + turned[0], even[pos][1] + turned[1]))
        second.append((even[pos][0] - turned[0], even[pos][1] - turned[1]))
    return first + second


HALVES = 2
SUBROWS = RADIX // HALVES


def pick_half(values, part):
    rows, lanes = values.shape
    return values.reshape(rows // RADIX, HALVES, SUBROWS, lanes)[:, part].reshape(-1, lanes)


def pack_half(part, volt_ref, first_send):
    half = LANES // 2
    block = 256

    def step(pos, carry):
        rows = pl.ds(pl.multiple_of(pos * block, block), block)
        out_rows = pl.ds(pl.multiple_of(pos * (block // HALVES), block // HALVES), block // HALVES)
        for dest in range(first_send.shape[1]):
            lanes = slice(dest * half, (dest + 1) * half)
            real = pick_half(volt_ref[0, rows, lanes].astype(jnp.float32), part)
            imag = pick_half(volt_ref[1, rows, lanes].astype(jnp.float32), part)
            first_send[part, dest, out_rows, :] = jnp.concatenate([real, imag], axis=1).astype(
                first_send.dtype
            )
        return carry

    lax.fori_loop(0, volt_ref.shape[1] // block, step, 0)


def far_first(me, parts, rank):
    down = parts - 1 - rank
    down = down - (me >= down).astype(jnp.int32)
    up = rank + (me <= rank).astype(jnp.int32)
    return jnp.where(me < parts // 2, down, up)


def turn_coefs(coef_ref, rows_ref):
    block = 256

    def step(pos, carry):
        lanes = pl.ds(pl.multiple_of(pos * block, block), block)
        out_rows = pl.ds(pl.multiple_of(pos * (block // HALVES), block // HALVES), block // HALVES)
        turned = jnp.transpose(coef_ref[:, lanes])
        for part in range(HALVES):
            rows_ref[part, out_rows, :] = pick_half(turned, part)
        return carry

    lax.fori_loop(0, coef_ref.shape[1] // block, step, 0)


def filter_dft(pair, part, data_ref, rows_ref, table_ref, filt_ref, mid_ref):
    taps_count = rows_ref.shape[2]
    rows_half = data_ref.shape[2]
    sub = rows_half // SUBROWS
    half = LANES // 2
    block = 128

    def filter_step(step, carry):
        rows = pl.ds(pl.multiple_of(step * block, block), block)
        coef = rows_ref[part, rows, :]
        low_lane = lax.broadcasted_iota(jnp.int32, (block, LANES), 1) < half
        samples = {}
        for time_pos in range(max(0, 2 * pair - taps_count + 1), 2 * pair + 2):
            samples[time_pos] = data_ref[part, time_pos, rows, :].astype(jnp.float32)
        sums = []
        for spectrum in (2 * pair, 2 * pair + 1):
            total = None
            for tap in range(taps_count):
                time_pos = spectrum - (taps_count - 1) + tap
                if time_pos < 0:
                    continue
                term = coef[:, tap : tap + 1] * samples[time_pos]
                total = term if total is None else total + term
            sums.append(total)
        filt_ref[0, rows, :] = jnp.where(low_lane, sums[0], pltpu.roll(sums[1], half, 1))
        filt_ref[1, rows, :] = jnp.where(low_lane, pltpu.roll(sums[0], half, 1), sums[1])
        return carry

    lax.fori_loop(0, rows_half // block, filter_step, 0)

    def dft_step(offset, carry):
        phase = part * SUBROWS + offset
        real_in = filt_ref[0, pl.ds(offset, sub, stride=SUBROWS), :]
        imag_in = filt_ref[1, pl.ds(offset, sub, stride=SUBROWS), :]
        high, low = split_halves(jnp.concatenate([real_in, imag_in], axis=0))

        def matrix(first):
            cos_m = table_ref[phase, first]
            sin_m = table_ref[phase, first + 1]
            return jnp.concatenate(
                [
                    jnp.concatenate([cos_m, sin_m], axis=1),
                    jnp.concatenate([-sin_m, cos_m], axis=1),
                ],
                axis=0,
            )

        big, small = matrix(0), matrix(2)
        total = jnp.dot(big, low, preferred_element_type=jnp.float32)
        total = total + jnp.dot(small, high, preferred_element_type=jnp.float32)
        total = total + jnp.dot(big, high, preferred_element_type=jnp.float32)
        mid_ref[pair, phase] = total
        return carry

    lax.fori_loop(0, SUBROWS, dft_step, 0, unroll=4)


def radix_pass(pair, mid_ref, send_ref):
    rounds, parts = send_ref.shape[1:3]
    rows_round = send_ref.shape[4]
    sub = mid_ref.shape[2] // 2
    splits = sub // rows_round
    groups = rounds // splits
    rows_step = 16

    for split in range(splits):

        def radix_step(step, carry):
            out_rows = pl.ds(pl.multiple_of(step * rows_step, rows_step), rows_step)
            start = pl.multiple_of(split * rows_round + step * rows_step, rows_step)
            values = [
                (
                    mid_ref[pair, phase, pl.ds(start, rows_step), :],
                    mid_ref[pair, phase, pl.ds(sub + start, rows_step), :],
                )
                for phase in range(RADIX)
            ]
            for group, (re, im) in enumerate(small_fft(values)):
                dest, turn = group // groups, group % groups * splits + split
                send_ref[pair, turn, dest, 0, out_rows, :] = re.astype(jnp.bfloat16)
                send_ref[pair, turn, dest, 1, out_rows, :] = im.astype(jnp.bfloat16)
            return carry

        lax.fori_loop(0, rows_round // rows_step, radix_step, 0)


def merge_round(pair, turn, col, recv_ref, out_ref):
    half = LANES // 2
    sources = recv_ref.shape[2]
    coarse_round = recv_ref.shape[4] // AVG
    for step in range(coarse_round):
        fine = pl.ds(step * AVG, AVG)
        rows = []
        for part in range(2):
            for spec in range(2):
                lanes = slice(spec * half, (spec + 1) * half)
                rows.append(
                    jnp.concatenate(
                        [recv_ref[pair, turn, src, part, fine, lanes] for src in range(sources)],
                        axis=1,
                    )
                )
        merged = jnp.concatenate(rows, axis=0)
        out_ref[col, turn * coarse_round + step, pair] = jnp.transpose(merged)


def exchange_kernel(
    parts,
    volt_ref,
    coef_ref,
    table_ref,
    out_ref,
    first_send,
    data_ref,
    rows_ref,
    filt_ref,
    mid_ref,
    send_ref,
    recv_ref,
    first_send_sem,
    first_recv_sem,
    turn_send_sem,
    turn_recv_sem,
    keep_sem,
    row_send_sem,
    row_recv_sem,
    own_sem,
):
    mesh_id = pl.DeviceIdType.MESH
    me = lax.axis_index("ft")
    col = lax.axis_index("bl")
    mate = col + 1 - 2 * lax.rem(col, 2)
    across = lax.rem(col + 2, 4)
    pairs, rounds = send_ref.shape[:2]
    coarse_round = recv_ref.shape[4] // AVG

    barrier = pltpu.get_barrier_semaphore()
    for shift in range(1, parts):
        pl.semaphore_signal(
            barrier, inc=1, device_id={"ft": lax.rem(me + shift, parts)}, device_id_type=mesh_id
        )
    for peer in (mate, across):
        pl.semaphore_signal(barrier, inc=1, device_id={"bl": peer}, device_id_type=mesh_id)

    def first_copy(part, dest):
        place = lax.rem(dest - me + parts, parts) - 1
        return pltpu.make_async_remote_copy(
            src_ref=first_send.at[part, dest],
            dst_ref=data_ref.at[part, me],
            send_sem=first_send_sem.at[part, place],
            recv_sem=first_recv_sem.at[part, place],
            device_id={"ft": dest},
            device_id_type=mesh_id,
        )

    def turn_copy(pair, turn, dest):
        place = lax.rem(dest - me + parts, parts) - 1
        return pltpu.make_async_remote_copy(
            src_ref=send_ref.at[pair, turn, dest],
            dst_ref=recv_ref.at[pair, turn, me],
            send_sem=turn_send_sem.at[pair, turn, place],
            recv_sem=turn_recv_sem.at[pair, turn, place],
            device_id={"ft": dest},
            device_id_type=mesh_id,
        )

    first = []
    for part in range(HALVES):
        pack_half(part, volt_ref, first_send)
        if part == 0:
            pl.semaphore_wait(barrier, parts + 1)
        for rank in range(parts - 1):
            first_copy(part, far_first(me, parts, rank)).start()
        copies = [first_copy(part, lax.rem(me + shift, parts)) for shift in range(1, parts)]
        keep = pltpu.make_async_copy(first_send.at[part, me], data_ref.at[part, me], own_sem.at[part])
        keep.start()
        first.append((copies, keep))
    turn_coefs(coef_ref, rows_ref)

    def arrive(part):
        copies, keep = first[part]
        keep.wait()
        for copy in copies:
            copy.wait_recv()

    for part in range(HALVES - 1):
        arrive(part)
        for pair in range(pairs):
            filter_dft(pair, part, data_ref, rows_ref, table_ref, filt_ref, mid_ref)
    arrive(HALVES - 1)

    turn_copies = {}

    def send_turn(pair, turn):
        for rank in range(parts - 1):
            turn_copy(pair, turn, far_first(me, parts, rank)).start()

    for pair in range(pairs):
        filter_dft(pair, HALVES - 1, data_ref, rows_ref, table_ref, filt_ref, mid_ref)
        radix_pass(pair, mid_ref, send_ref)
        for turn in range(rounds):
            if pair * rounds + turn < WINDOW:
                send_turn(pair, turn)
            copies = [turn_copy(pair, turn, lax.rem(me + shift, parts)) for shift in range(1, parts)]
            keep = pltpu.make_async_copy(
                send_ref.at[pair, turn, me], recv_ref.at[pair, turn, me], keep_sem.at[pair, turn]
            )
            keep.start()
            turn_copies[pair, turn] = (copies, keep)

    def row_copy(kind, pair, turn, src, block, peer):
        rows = pl.ds(turn * coarse_round, coarse_round)
        return pltpu.make_async_remote_copy(
            src_ref=src,
            dst_ref=out_ref.at[block, rows, pair],
            send_sem=row_send_sem.at[kind, pair, turn],
            recv_sem=row_recv_sem.at[kind, pair, turn],
            device_id={"bl": peer},
            device_id_type=mesh_id,
        )

    order = [(pair, turn) for pair in range(pairs) for turn in range(rounds)]
    across_copies, late = {}, []

    def relay(pair, turn):
        across_copies[pair, turn].wait_recv()
        rows = pl.ds(turn * coarse_round, coarse_round)
        copy = row_copy(2, pair, turn, out_ref.at[across, rows, pair], across, mate)
        copy.start()
        late.append(copy)

    lag = 3
    for count, (pair, turn) in enumerate(order):
        copies, keep = turn_copies[pair, turn]
        keep.wait()
        for copy in copies:
            copy.wait_recv()
        if count + WINDOW < len(order):
            send_turn(*order[count + WINDOW])
        merge_round(pair, turn, col, recv_ref, out_ref)
        rows = pl.ds(turn * coarse_round, coarse_round)
        source = out_ref.at[col, rows, pair]
        far = row_copy(0, pair, turn, source, col, across)
        far.start()
        near = row_copy(1, pair, turn, source, col, mate)
        near.start()
        across_copies[pair, turn] = far
        late.append(near)
        if count >= lag:
            relay(*order[count - lag])
    for position in order[len(order) - lag :]:
        relay(*position)
    for copy in late:
        copy.wait()
    for copy in across_copies.values():
        copy.wait_send()
    for copies, _ in turn_copies.values():
        for copy in copies:
            copy.wait_send()
    for copies, _ in first:
        for copy in copies:
            copy.wait_send()


def exchange(voltages, coefs, table, parts, blocks):
    _, chan_count, rows_here = voltages.shape
    sub = chan_count // RADIX
    pairs = parts // 2
    rows_round = AVG
    rounds = RADIX // parts * (sub // rows_round)
    coarse_here = chan_count // parts // AVG
    depth = 4 * AVG
    vmem = pl.BlockSpec(memory_space=pltpu.VMEM)
    dma = pltpu.SemaphoreType.DMA
    return pl.pallas_call(
        functools.partial(exchange_kernel, parts),
        in_specs=[vmem] * 3,
        out_specs=vmem,
        out_shape=pltpu.VMEM((blocks, coarse_here, pairs, rows_here, depth), jnp.bfloat16),
        scratch_shapes=[
            pltpu.VMEM((HALVES, parts, chan_count // HALVES, LANES), jnp.bfloat16),
            pltpu.VMEM((HALVES, parts, chan_count // HALVES, LANES), jnp.bfloat16),
            pltpu.VMEM((HALVES, chan_count // HALVES, coefs.shape[0]), jnp.float32),
            pltpu.VMEM((2, chan_count // HALVES, LANES), jnp.float32),
            pltpu.VMEM((pairs, RADIX, 2 * sub, LANES), jnp.float32),
            pltpu.VMEM((pairs, rounds, parts, 2, rows_round, LANES), jnp.bfloat16),
            pltpu.VMEM((pairs, rounds, parts, 2, rows_round, LANES), jnp.bfloat16),
            dma((HALVES, parts - 1)),
            dma((HALVES, parts - 1)),
            dma((pairs, rounds, parts - 1)),
            dma((pairs, rounds, parts - 1)),
            dma((pairs, rounds)),
            dma((3, pairs, rounds)),
            dma((3, pairs, rounds)),
            dma((HALVES,)),
        ],
        compiler_params=pltpu.CompilerParams(
            collective_id=0, has_side_effects=True, vmem_limit_bytes=40 * 2**20
        ),
        name="exchange",
    )(voltages, coefs, table)


def plan_slots(ids_ref, owner_ref, slot_ref, blocks):
    my_index = lax.axis_index("bl")
    slot_cap = slot_ref.shape[1]
    for slot in range(slot_cap):
        for row in range(3):
            slot_ref[row, slot] = 0
    shard_of = []
    for label in range(blocks):
        shard = jnp.int32(0)
        for pos in range(blocks):
            shard = shard + jnp.where(ids_ref[pos] == label, pos, 0)
        shard_of.append(shard)
    count = jnp.int32(0)
    pairs = [(i, j) for i in range(blocks) for j in range(i, blocks)]
    for tile, (first_id, second_id) in enumerate(pairs):
        mine = (owner_ref[tile] == my_index) & (count < slot_cap)

        @pl.when(mine)
        def _():
            slot_ref[0, count] = shard_of[first_id]
            slot_ref[1, count] = shard_of[second_id]
            slot_ref[2, count] = 1

        count = count + mine.astype(jnp.int32)


def tiles_kernel(norm_scale, ids_ref, owner_ref, data_ref, out_ref, slot_ref):
    _, _, pairs, _, depth = data_ref.shape
    coarse = pl.program_id(0)

    @pl.when(coarse == 0)
    def _():
        plan_slots(ids_ref, owner_ref, slot_ref, data_ref.shape[0])

    half = depth // 2
    contract = (((1,), (1,)), ((), ()))
    for slot in range(out_ref.shape[2]):
        scale = jnp.where(slot_ref[2, slot] > 0, norm_scale, 0.0)
        real, imag = None, None
        for pair in range(pairs):
            row = data_ref[slot_ref[0, slot], coarse, pair]
            col = data_ref[slot_ref[1, slot], coarse, pair]
            swapped = jnp.concatenate([row[:, half:], -row[:, :half]], axis=1)
            first = lax.dot_general(row, col, contract, preferred_element_type=jnp.float32)
            second = lax.dot_general(swapped, col, contract, preferred_element_type=jnp.float32)
            real = first if real is None else real + first
            imag = second if imag is None else imag + second
        out_ref[0, 0, slot] = real * scale
        out_ref[1, 0, slot] = imag * scale


def make_tiles(block_ids, tile_owner, gathered, norm_scale):
    blocks, coarse_here, pairs, rows_here, depth = gathered.shape
    tile_count = blocks * (blocks + 1) // 2
    slot_cap = 2 * tile_count // blocks
    return pl.pallas_call(
        functools.partial(tiles_kernel, norm_scale),
        grid_spec=pltpu.PrefetchScalarGridSpec(
            num_scalar_prefetch=2,
            grid=(coarse_here,),
            in_specs=[pl.BlockSpec(memory_space=pltpu.VMEM)],
            out_specs=pl.BlockSpec(
                (2, 1, slot_cap, rows_here, rows_here), lambda c, *_: (0, c, 0, 0, 0)
            ),
            scratch_shapes=[pltpu.SMEM((3, slot_cap), jnp.int32)],
        ),
        out_shape=jax.ShapeDtypeStruct((2, coarse_here, slot_cap, rows_here, rows_here), jnp.float32),
        compiler_params=pltpu.CompilerParams(vmem_limit_bytes=40 * 2**20),
        name="tiles",
    )(block_ids, tile_owner, gathered)


def per_device_packed(voltages, coefs, block_ids, tile_owner):
    parts = lax.axis_size("ft")
    table = jnp.asarray(dft_constants(coefs.shape[1]))
    gathered = exchange(voltages, coefs, table, parts, lax.axis_size("bl"))
    return make_tiles(block_ids, tile_owner, gathered, 1.0 / (AVG * parts))


def per_device(voltages, coefs, block_ids, tile_owner):
    chan_count = coefs.shape[1]
    parts = lax.axis_size("ft")
    fits = (
        voltages.shape[1] == chan_count
        and parts % 2 == 0
        and RADIX % parts == 0
        and voltages.shape[2] == parts * LANES // 2
        and chan_count == RADIX * LANES
        and (chan_count // RADIX) % AVG == 0
        and lax.axis_size("bl") == 4
    )
    if fits:
        return per_device_packed(voltages, coefs, block_ids, tile_owner)
    return per_device_general(voltages, coefs, block_ids, tile_owner)


def solution(mesh):
    return jax.shard_map(
        per_device,
        mesh=mesh,
        in_specs=(P(None, ("grp", "ft"), "bl"), P(), P(), P("grp")),
        out_specs=P(None, ("grp", "ft"), "bl", None, None),
        check_vma=False,
    )
```

```python
import functools
import math

import jax
import jax.numpy as jnp
import numpy as np
from jax import lax
from jax.experimental import pallas as pl
from jax.experimental.pallas import tpu as pltpu
from jax.sharding import PartitionSpec as P

AVG = 64


def tile_product(row_part, col_part, norm_scale):
    products = jnp.einsum(
        "pscax,qscay->cpqxy", row_part, col_part, preferred_element_type=jnp.float32
    )
    real_part = products[:, 0, 0] + products[:, 1, 1]
    imag_part = products[:, 1, 0] - products[:, 0, 1]
    return jnp.stack([real_part, imag_part]) * norm_scale


def dft_tables(order_len):
    steps_one = jnp.arange(order_len, dtype=jnp.int32)
    phase_grid = steps_one[:, None] * steps_one[None, :] % order_len
    angles = phase_grid.astype(jnp.float32) * (2.0 * math.pi / order_len)
    return (jnp.cos(angles), jnp.sin(angles))


def transform(filtered):
    per_dev = filtered.shape[1]
    chan_count = filtered.shape[2]
    rows_here = filtered.shape[3]
    outer_len = math.isqrt(chan_count)
    while chan_count % outer_len != 0:
        outer_len = outer_len - 1
    inner_len = chan_count // outer_len
    highest = lax.Precision.HIGHEST
    reshaped = filtered.reshape(2, per_dev, outer_len, inner_len, rows_here)
    real_in = reshaped[0]
    imag_in = reshaped[1]
    cos_outer, sin_outer = dft_tables(outer_len)
    section_re = jnp.einsum("snkb,nm->smkb", real_in, cos_outer, precision=highest) + jnp.einsum(
        "snkb,nm->smkb", imag_in, sin_outer, precision=highest
    )
    section_im = jnp.einsum("snkb,nm->smkb", imag_in, cos_outer, precision=highest) - jnp.einsum(
        "snkb,nm->smkb", real_in, sin_outer, precision=highest
    )
    twiddle_grid = (
        jnp.arange(outer_len, dtype=jnp.int32)[:, None]
        * jnp.arange(inner_len, dtype=jnp.int32)[None, :]
        % chan_count
    )
    twiddle_angles = twiddle_grid.astype(jnp.float32) * (2.0 * math.pi / chan_count)
    cos_twiddle = jnp.cos(twiddle_angles)[None, :, :, None]
    sin_twiddle = jnp.sin(twiddle_angles)[None, :, :, None]
    rot_re = section_re * cos_twiddle + section_im * sin_twiddle
    rot_im = section_im * cos_twiddle - section_re * sin_twiddle
    cos_inner, sin_inner = dft_tables(inner_len)
    final_re = jnp.einsum("smkb,kq->sqmb", rot_re, cos_inner, precision=highest) + jnp.einsum(
        "smkb,kq->sqmb", rot_im, sin_inner, precision=highest
    )
    final_im = jnp.einsum("smkb,kq->sqmb", rot_im, cos_inner, precision=highest) - jnp.einsum(
        "smkb,kq->sqmb", rot_re, sin_inner, precision=highest
    )
    stacked = jnp.stack([final_re, final_im]).reshape(2, per_dev, chan_count, rows_here)
    return (stacked * (1.0 / math.sqrt(chan_count))).astype(jnp.bfloat16)


def apply_taps(window, coef_part, taps_count, out_len):
    filtered = jnp.zeros((2, out_len, window.shape[2], window.shape[3]), jnp.float32)
    for tap_index in range(taps_count):
        filtered = filtered + coef_part[tap_index][None, None, :, None] * window[
            :, tap_index : tap_index + out_len
        ].astype(jnp.float32)
    return filtered


def per_device_general(voltages, coefs, block_ids, tile_owner):
    taps_count = coefs.shape[0]
    chan_count = coefs.shape[1]
    rows_here = voltages.shape[2]
    per_dev = voltages.shape[1] // chan_count
    volt_blocks = voltages.reshape(2, per_dev, chan_count, rows_here)
    phase_block = lax.all_to_all(volt_blocks, "ft", split_axis=2, concat_axis=1, tiled=True)
    spectra_count = phase_block.shape[1]
    phase_here = phase_block.shape[2]
    coef_part = lax.dynamic_slice_in_dim(coefs, lax.axis_index("ft") * phase_here, phase_here, 1)
    zero_front = jnp.zeros((2, taps_count - 1, phase_here, rows_here), phase_block.dtype)
    long_window = jnp.concatenate([zero_front, phase_block], axis=1)
    phase_filtered = apply_taps(long_window, coef_part, taps_count, spectra_count)
    filtered = lax.all_to_all(phase_filtered, "ft", split_axis=1, concat_axis=2, tiled=True)
    spectra = transform(filtered)
    turned = lax.all_to_all(spectra, "ft", split_axis=2, concat_axis=1, tiled=True)
    spectra_all = turned.shape[1]
    chan_here = turned.shape[2]
    coarse_here = chan_here // AVG
    coarse_view = turned.reshape(2, spectra_all, coarse_here, AVG, rows_here)
    norm_scale = 1.0 / (AVG * spectra_all)
    block_count = lax.axis_size("bl")
    my_index = lax.axis_index("bl")
    tile_count = block_count * (block_count + 1) // 2
    slot_cap = 2 * tile_count // block_count
    row_table = jnp.asarray(
        np.array(
            [
                first_id
                for first_id in range(block_count)
                for second_id in range(first_id, block_count)
            ],
            dtype=np.int32,
        )
    )
    col_table = jnp.asarray(
        np.array(
            [
                second_id
                for first_id in range(block_count)
                for second_id in range(first_id, block_count)
            ],
            dtype=np.int32,
        )
    )
    tile_pos = jnp.arange(tile_count, dtype=jnp.int32)
    same_owner = tile_owner[None, :] == tile_owner[:, None]
    before_mask = tile_pos[None, :] < tile_pos[:, None]
    slot_rank = jnp.sum((same_owner & before_mask).astype(jnp.int32), axis=1)
    labels = jnp.arange(block_count, dtype=jnp.int32)
    shard_of = jnp.sum(jnp.where(block_ids[None, :] == labels[:, None], labels[None, :], 0), axis=1)
    gathered = lax.all_gather(coarse_view[None], "bl", axis=0, tiled=True)
    mine_mask = tile_owner == my_index
    own_count = jnp.sum(mine_mask.astype(jnp.int32))
    slot_steps = jnp.arange(slot_cap, dtype=jnp.int32)
    slot_tile = jnp.sum(
        jnp.where(
            mine_mask[None, :] & (slot_rank[None, :] == slot_steps[:, None]), tile_pos[None, :], 0
        ),
        axis=1,
    )

    def one_tile(slot_pos, result_tiles):
        tile_id = slot_tile[slot_pos]
        row_block = gathered[shard_of[row_table[tile_id]]]
        col_block = gathered[shard_of[col_table[tile_id]]]
        tile = tile_product(row_block, col_block, norm_scale)
        return lax.dynamic_update_slice(result_tiles, tile[:, :, None], (0, 0, slot_pos, 0, 0))

    empty_tiles = jnp.zeros((2, coarse_here, slot_cap, rows_here, rows_here), jnp.float32)
    return lax.fori_loop(0, own_count, one_tile, empty_tiles)


LANES = 128
RADIX = 16
WINDOW = 3
LAG = 3
SPARE = 4


def split_halves(values):
    high = values.astype(jnp.bfloat16)
    low = (values - high.astype(jnp.float32)).astype(jnp.bfloat16)
    return high, low


def dft_constants(chan_count):
    rows = chan_count // RADIX
    m_grid = np.arange(rows, dtype=np.int64)[None, :, None]
    n_grid = RADIX * np.arange(rows, dtype=np.int64)[None, None, :] + np.arange(RADIX)[:, None, None]
    angles = (m_grid * n_grid % chan_count) * (2.0 * np.pi / chan_count)
    scale = 1.0 / math.sqrt(chan_count)
    parts = []
    for table in (np.cos(angles) * scale, np.sin(angles) * scale):
        high = table.astype(jnp.bfloat16)
        parts.append(high)
        parts.append((table - high.astype(np.float64)).astype(jnp.bfloat16))
    return np.stack([parts[0], parts[2], parts[1], parts[3]], axis=1)


def turn_values(value, step, count):
    re, im = value
    step = step % count
    if step == 0:
        return value
    if 4 * step == count:
        return im, -re
    if 2 * step == count:
        return -re, -im
    if 8 * step == count:
        half = np.float32(math.sqrt(0.5))
        return (re + im) * half, (im - re) * half
    if 8 * step == 3 * count:
        half = np.float32(math.sqrt(0.5))
        return (im - re) * half, -(re + im) * half
    angle = 2.0 * math.pi * step / count
    cos_v, sin_v = np.float32(math.cos(angle)), np.float32(math.sin(angle))
    return re * cos_v + im * sin_v, im * cos_v - re * sin_v


def small_fft(values):
    count = len(values)
    if count == 1:
        return values
    even = small_fft(values[0::2])
    odd = small_fft(values[1::2])
    first, second = [], []
    for pos in range(count // 2):
        turned = turn_values(odd[pos], pos, count)
        first.append((even[pos][0] + turned[0], even[pos][1] + turned[1]))
        second.append((even[pos][0] - turned[0], even[pos][1] - turned[1]))
    return first + second


CHUNKS = 2
SPECTRA = 4
GROUP = LANES // SPECTRA


def pack_chunk(chunk, volt_ref, first_send):
    rows_half = first_send.shape[2]
    tile = slice(chunk * LANES, (chunk + 1) * LANES)
    block = 64

    def step(pos, carry):
        rows = pl.ds(pl.multiple_of(pos * block, block), block)
        late = pl.ds(pl.multiple_of(rows_half + pos * block, block), block)
        pieces = [volt_ref[part, place, tile] for place in (rows, late) for part in range(2)]
        for dest in range(first_send.shape[1]):
            lanes = slice(dest * GROUP, (dest + 1) * GROUP)
            first_send[chunk, dest, rows, :] = jnp.concatenate(
                [piece[:, lanes] for piece in pieces], axis=1
            )
        return carry

    lax.fori_loop(0, rows_half // block, step, 0)


def far_first(me, parts, rank):
    down = parts - 1 - rank
    down = down - (me >= down).astype(jnp.int32)
    up = rank + (me <= rank).astype(jnp.int32)
    return jnp.where(me < parts // 2, down, up)


def widen_coefs(coef_ref, wide_ref):
    taps_count = coef_ref.shape[0]
    lags, rows_half, _ = wide_ref.shape
    block = 128

    def step(pos, carry):
        rows = pl.ds(pl.multiple_of(pos * block, block), block)
        late = pl.ds(pl.multiple_of(rows_half + pos * block, block), block)
        first = jnp.transpose(coef_ref[:, rows])
        second = jnp.transpose(coef_ref[:, late])
        low_lane = lax.broadcasted_iota(jnp.int32, (block, LANES), 1) < LANES // 2
        for lag in range(lags):
            tap = taps_count - 1 - lag
            wide_ref[lag, rows, :] = jnp.where(
                low_lane, first[:, tap : tap + 1], second[:, tap : tap + 1]
            )
        return carry

    lax.fori_loop(0, rows_half // block, step, 0)


def swap_groups(values):
    lane = lax.broadcasted_iota(jnp.int32, values[0].shape, 1)
    low = lane < 2 * GROUP
    even = lane % (2 * GROUP) < GROUP
    mixed = [None] * 4
    for pos in range(2):
        one, two = values[pos], values[pos + 2]
        mixed[pos] = jnp.where(low, one, pltpu.roll(two, 2 * GROUP, 1))
        mixed[pos + 2] = jnp.where(low, pltpu.roll(one, 2 * GROUP, 1), two)
    result = [None] * 4
    for pos in (0, 2):
        one, two = mixed[pos], mixed[pos + 1]
        result[pos] = jnp.where(even, one, pltpu.roll(two, GROUP, 1))
        result[pos + 1] = jnp.where(even, pltpu.roll(one, 3 * GROUP, 1), two)
    return result


def filter_chunk(chunk, first, count, data_ref, wide_ref, filt_ref):
    lags = wide_ref.shape[0]
    rows_half = data_ref.shape[2]
    block = 16

    def step(pos, carry):
        rows = pl.ds(pl.multiple_of(pos * block, block), block)
        late = pl.ds(pl.multiple_of(rows_half + pos * block, block), block)
        samples = [data_ref[chunk, src, rows, :].astype(jnp.float32) for src in range(SPECTRA)]
        coef = [wide_ref[lag, rows, :] for lag in range(lags)]
        sums = []
        for spectrum in range(SPECTRA):
            total = None
            for time_pos in range(max(0, spectrum - lags + 1), spectrum + 1):
                term = coef[spectrum - time_pos] * samples[time_pos]
                total = term if total is None else total + term
            sums.append(total)
        re_first, im_first, re_late, im_late = swap_groups(sums)
        filt_ref[0, rows, :] = re_first
        filt_ref[1, rows, :] = im_first
        filt_ref[0, late, :] = re_late
        filt_ref[1, late, :] = im_late
        return carry

    lax.fori_loop(first // block, (first + count) // block, step, 0, unroll=2)


def dft_chunk(chunk, first, count, table_ref, filt_ref, mid_ref):
    sub = filt_ref.shape[1] // RADIX

    def dft_step(step, carry):
        phase = first + step
        real_in = filt_ref[0, pl.ds(phase, sub, stride=RADIX), :]
        imag_in = filt_ref[1, pl.ds(phase, sub, stride=RADIX), :]
        high, low = split_halves(jnp.concatenate([real_in, imag_in], axis=0))

        def matrix(pick):
            cos_m = table_ref[phase, pick]
            sin_m = table_ref[phase, pick + 1]
            return jnp.concatenate(
                [
                    jnp.concatenate([cos_m, sin_m], axis=1),
                    jnp.concatenate([-sin_m, cos_m], axis=1),
                ],
                axis=0,
            )

        big, small = matrix(0), matrix(2)
        total = jnp.dot(big, low, preferred_element_type=jnp.float32)
        total = total + jnp.dot(small, high, preferred_element_type=jnp.float32)
        total = total + jnp.dot(big, high, preferred_element_type=jnp.float32)
        mid_ref[chunk, phase] = total
        return carry

    lax.fori_loop(0, count, dft_step, 0, unroll=4)


def radix_pass(chunk, mid_ref, send_ref):
    rounds, parts = send_ref.shape[1:3]
    rows_round = send_ref.shape[4]
    sub = mid_ref.shape[2] // 2
    splits = sub // rows_round
    groups = rounds // splits
    rows_step = 16

    for split in range(splits):

        def radix_step(step, carry):
            out_rows = pl.ds(pl.multiple_of(step * rows_step, rows_step), rows_step)
            start = pl.multiple_of(split * rows_round + step * rows_step, rows_step)
            values = [
                (
                    mid_ref[chunk, phase, pl.ds(start, rows_step), :],
                    mid_ref[chunk, phase, pl.ds(sub + start, rows_step), :],
                )
                for phase in range(RADIX)
            ]
            for group, (re, im) in enumerate(small_fft(values)):
                dest, turn = group // groups, group % groups * splits + split
                send_ref[chunk, turn, dest, 0, out_rows, :] = re.astype(jnp.bfloat16)
                send_ref[chunk, turn, dest, 1, out_rows, :] = im.astype(jnp.bfloat16)
            return carry

        lax.fori_loop(0, rows_round // rows_step, radix_step, 0)


def merge_round(chunk, turn, col, recv_ref, out_ref):
    coarse_round = recv_ref.shape[4] // AVG
    for step in range(coarse_round):
        fine = pl.ds(step * AVG, AVG)
        for src in range(recv_ref.shape[2]):
            both = [recv_ref[chunk, turn, src, part, fine, :] for part in range(2)]
            turned = jnp.transpose(jnp.concatenate(both, axis=0))
            for spectrum in range(SPECTRA):
                depth = pl.ds(spectrum * 2 * AVG, 2 * AVG)
                out_ref[
                    col, turn * coarse_round + step, chunk, pl.ds(src * GROUP, GROUP), depth
                ] = turned[spectrum * GROUP : (spectrum + 1) * GROUP]


def exchange_kernel(
    parts,
    volt_in,
    coef_in,
    table_in,
    out_ref,
    volt_ref,
    coef_ref,
    table_ref,
    first_send,
    data_ref,
    wide_ref,
    filt_ref,
    mid_ref,
    send_ref,
    recv_ref,
    load_sem,
    first_send_sem,
    first_recv_sem,
    turn_send_sem,
    turn_recv_sem,
    keep_sem,
    row_send_sem,
    row_recv_sem,
    own_sem,
):
    mesh_id = pl.DeviceIdType.MESH
    me = lax.axis_index("ft")
    col = lax.axis_index("bl")
    mate = col + 1 - 2 * lax.rem(col, 2)
    across = lax.rem(col + 2, 4)
    rounds = send_ref.shape[1]
    coarse_round = recv_ref.shape[4] // AVG

    barrier = pltpu.get_barrier_semaphore()
    for shift in range(1, parts):
        pl.semaphore_signal(
            barrier, inc=1, device_id={"ft": lax.rem(me + shift, parts)}, device_id_type=mesh_id
        )
    for peer in (mate, across):
        pl.semaphore_signal(barrier, inc=1, device_id={"bl": peer}, device_id_type=mesh_id)

    volt_loads = []
    for chunk in range(CHUNKS):
        tile = pl.ds(chunk * LANES, LANES)
        volt_loads.append(
            pltpu.make_async_copy(
                volt_in.at[:, :, tile], volt_ref.at[:, :, tile], load_sem.at[chunk]
            )
        )
    coef_load = pltpu.make_async_copy(coef_in, coef_ref, load_sem.at[CHUNKS])
    table_load = pltpu.make_async_copy(table_in, table_ref, load_sem.at[CHUNKS + 1])
    for copy in (*volt_loads, coef_load, table_load):
        copy.start()

    def first_copy(chunk, dest):
        place = lax.rem(dest - me + parts, parts) - 1
        return pltpu.make_async_remote_copy(
            src_ref=first_send.at[chunk, dest],
            dst_ref=data_ref.at[chunk, me],
            send_sem=first_send_sem.at[chunk, place],
            recv_sem=first_recv_sem.at[chunk, place],
            device_id={"ft": dest},
            device_id_type=mesh_id,
        )

    def turn_copy(chunk, turn, dest):
        place = lax.rem(dest - me + parts, parts) - 1
        return pltpu.make_async_remote_copy(
            src_ref=send_ref.at[chunk, turn, dest],
            dst_ref=recv_ref.at[chunk, turn, me],
            send_sem=turn_send_sem.at[chunk, turn, place],
            recv_sem=turn_recv_sem.at[chunk, turn, place],
            device_id={"ft": dest},
            device_id_type=mesh_id,
        )

    first = []
    for chunk in range(CHUNKS):
        volt_loads[chunk].wait()
        pack_chunk(chunk, volt_ref, first_send)
        if chunk == 0:
            pl.semaphore_wait(barrier, parts + 1)
        for rank in range(parts - 1):
            first_copy(chunk, far_first(me, parts, rank)).start()
        copies = [first_copy(chunk, lax.rem(me + shift, parts)) for shift in range(1, parts)]
        keep = pltpu.make_async_copy(
            first_send.at[chunk, me], data_ref.at[chunk, me], own_sem.at[chunk]
        )
        keep.start()
        first.append((copies, keep))
    coef_load.wait()
    widen_coefs(coef_ref, wide_ref)
    table_load.wait()

    def arrive(chunk):
        copies, keep = first[chunk]
        keep.wait()
        for copy in copies:
            copy.wait_recv()

    def sections(chunk):
        rows_half = data_ref.shape[2]
        for pos in range(2):
            filter_chunk(
                chunk, pos * rows_half // 2, rows_half // 2, data_ref, wide_ref, filt_ref
            )
            yield
        for pos in range(2):
            dft_chunk(chunk, pos * RADIX // 2, RADIX // 2, table_ref, filt_ref, mid_ref)
            yield
        radix_pass(chunk, mid_ref, send_ref)
        yield

    turn_copies = {}

    def send_turn(chunk, turn):
        for rank in range(parts - 1):
            turn_copy(chunk, turn, far_first(me, parts, rank)).start()
        copies = [turn_copy(chunk, turn, lax.rem(me + shift, parts)) for shift in range(1, parts)]
        keep = pltpu.make_async_copy(
            send_ref.at[chunk, turn, me], recv_ref.at[chunk, turn, me], keep_sem.at[chunk, turn]
        )
        keep.start()
        turn_copies[chunk, turn] = (copies, keep)

    def row_copy(kind, chunk, turn, src, block, peer):
        rows = pl.ds(turn * coarse_round, coarse_round)
        return pltpu.make_async_remote_copy(
            src_ref=src,
            dst_ref=out_ref.at[block, rows, chunk],
            send_sem=row_send_sem.at[kind, chunk, turn],
            recv_sem=row_recv_sem.at[kind, chunk, turn],
            device_id={"bl": peer},
            device_id_type=mesh_id,
        )

    order = [(chunk, turn) for chunk in range(CHUNKS) for turn in range(rounds)]
    across_copies, late = {}, []

    def relay(chunk, turn):
        across_copies[chunk, turn].wait_recv()
        rows = pl.ds(turn * coarse_round, coarse_round)
        copy = row_copy(2, chunk, turn, out_ref.at[across, rows, chunk], across, mate)
        copy.start()
        late.append(copy)

    def advance(count):
        chunk, turn = order[count]
        copies, keep = turn_copies[chunk, turn]
        keep.wait()
        for copy in copies:
            copy.wait_recv()
        if count + WINDOW < len(order):
            send_turn(*order[count + WINDOW])
        merge_round(chunk, turn, col, recv_ref, out_ref)
        rows = pl.ds(turn * coarse_round, coarse_round)
        source = out_ref.at[col, rows, chunk]
        far = row_copy(0, chunk, turn, source, col, across)
        far.start()
        near = row_copy(1, chunk, turn, source, col, mate)
        near.start()
        across_copies[chunk, turn] = far
        late.append(near)
        if count >= LAG:
            relay(*order[count - LAG])

    done = 0
    for chunk in range(CHUNKS):
        arrive(chunk)
        for _ in sections(chunk):
            if chunk > 0:
                advance(done)
                done += 1
        if chunk == 0:
            for position in order[:WINDOW]:
                send_turn(*position)
    for count in range(done, len(order)):
        advance(count)
    for position in order[len(order) - LAG :]:
        relay(*position)
    for copy in late:
        copy.wait()
    for copy in across_copies.values():
        copy.wait_send()
    for copies, _ in turn_copies.values():
        for copy in copies:
            copy.wait_send()
    for copies, _ in first:
        for copy in copies:
            copy.wait_send()


def exchange(voltages, coefs, table, parts, blocks):
    _, chan_count, rows_here = voltages.shape
    sub = chan_count // RADIX
    rows_round = AVG
    rounds = RADIX // parts * (sub // rows_round)
    coarse_here = chan_count // parts // AVG
    depth = SPECTRA * 2 * AVG
    rows_half = chan_count // 2
    lags = min(SPECTRA, coefs.shape[0])
    dma = pltpu.SemaphoreType.DMA
    return pl.pallas_call(
        functools.partial(exchange_kernel, parts),
        in_specs=[pl.BlockSpec(memory_space=pltpu.HBM)] * 3,
        out_specs=pl.BlockSpec(memory_space=pltpu.VMEM),
        out_shape=pltpu.VMEM((blocks + SPARE, coarse_here, CHUNKS, LANES, depth), jnp.bfloat16),
        scratch_shapes=[
            pltpu.VMEM(voltages.shape, voltages.dtype),
            pltpu.VMEM(coefs.shape, coefs.dtype),
            pltpu.VMEM(table.shape, table.dtype),
            pltpu.VMEM((CHUNKS, parts, rows_half, LANES), jnp.bfloat16),
            pltpu.VMEM((CHUNKS, parts, rows_half, LANES), jnp.bfloat16),
            pltpu.VMEM((lags, rows_half, LANES), jnp.float32),
            pltpu.VMEM((2, chan_count, LANES), jnp.float32),
            pltpu.VMEM((CHUNKS, RADIX, 2 * sub, LANES), jnp.float32),
            pltpu.VMEM((CHUNKS, rounds, parts, 2, rows_round, LANES), jnp.bfloat16),
            pltpu.VMEM((CHUNKS, rounds, parts, 2, rows_round, LANES), jnp.bfloat16),
            dma((CHUNKS + 2,)),
            dma((CHUNKS, parts - 1)),
            dma((CHUNKS, parts - 1)),
            dma((CHUNKS, rounds, parts - 1)),
            dma((CHUNKS, rounds, parts - 1)),
            dma((CHUNKS, rounds)),
            dma((3, CHUNKS, rounds)),
            dma((3, CHUNKS, rounds)),
            dma((CHUNKS,)),
        ],
        compiler_params=pltpu.CompilerParams(
            collective_id=0, has_side_effects=True, vmem_limit_bytes=44 * 2**20
        ),
        name="exchange",
    )(voltages, coefs, table)


def plan_slots(ids_ref, owner_ref, slot_ref, blocks):
    my_index = lax.axis_index("bl")
    slot_cap = slot_ref.shape[1]
    for slot in range(slot_cap):
        for row in range(3):
            slot_ref[row, slot] = 0
    shard_of = []
    for label in range(blocks):
        shard = jnp.int32(0)
        for pos in range(blocks):
            shard = shard + jnp.where(ids_ref[pos] == label, pos, 0)
        shard_of.append(shard)
    count = jnp.int32(0)
    pairs = [(i, j) for i in range(blocks) for j in range(i, blocks)]
    for tile, (first_id, second_id) in enumerate(pairs):
        mine = (owner_ref[tile] == my_index) & (count < slot_cap)

        @pl.when(mine)
        def _():
            slot_ref[0, count] = shard_of[first_id]
            slot_ref[1, count] = shard_of[second_id]
            slot_ref[2, count] = 1

        count = count + mine.astype(jnp.int32)


def tiles_kernel(norm_scale, ids_ref, owner_ref, data_ref, out_ref, slot_ref):
    depth = data_ref.shape[4]
    coarse = pl.program_id(0)

    @pl.when(coarse == 0)
    def _():
        plan_slots(ids_ref, owner_ref, slot_ref, ids_ref.shape[0])

    contract = (((1,), (1,)), ((), ()))
    for slot in range(out_ref.shape[2]):
        scale = jnp.where(slot_ref[2, slot] > 0, norm_scale, 0.0)
        row = data_ref[slot_ref[0, slot], coarse].reshape(-1, depth)
        col = data_ref[slot_ref[1, slot], coarse].reshape(-1, depth)
        pieces = [row[:, pos : pos + AVG] for pos in range(0, depth, AVG)]
        swapped = jnp.concatenate(
            [-pieces[pos - 1] if pos % 2 else pieces[pos + 1] for pos in range(len(pieces))], axis=1
        )
        real = lax.dot_general(row, col, contract, preferred_element_type=jnp.float32)
        imag = lax.dot_general(swapped, col, contract, preferred_element_type=jnp.float32)
        out_ref[0, 0, slot] = real * scale
        out_ref[1, 0, slot] = imag * scale


def make_tiles(block_ids, tile_owner, gathered, norm_scale):
    _, coarse_here, chunks, lanes, _ = gathered.shape
    blocks = block_ids.shape[0]
    rows_here = chunks * lanes
    tile_count = blocks * (blocks + 1) // 2
    slot_cap = 2 * tile_count // blocks
    return pl.pallas_call(
        functools.partial(tiles_kernel, norm_scale),
        grid_spec=pltpu.PrefetchScalarGridSpec(
            num_scalar_prefetch=2,
            grid=(coarse_here,),
            in_specs=[pl.BlockSpec(memory_space=pltpu.VMEM)],
            out_specs=pl.BlockSpec(
                (2, 1, slot_cap, rows_here, rows_here), lambda c, *_: (0, c, 0, 0, 0)
            ),
            scratch_shapes=[pltpu.SMEM((3, slot_cap), jnp.int32)],
        ),
        out_shape=jax.ShapeDtypeStruct((2, coarse_here, slot_cap, rows_here, rows_here), jnp.float32),
        compiler_params=pltpu.CompilerParams(vmem_limit_bytes=24 * 2**20),
        name="tiles",
    )(block_ids, tile_owner, gathered)


def per_device_packed(voltages, coefs, block_ids, tile_owner):
    parts = lax.axis_size("ft")
    table = jnp.asarray(dft_constants(coefs.shape[1]))
    gathered = exchange(voltages, coefs, table, parts, lax.axis_size("bl"))
    return make_tiles(block_ids, tile_owner, gathered, 1.0 / (AVG * parts))


def per_device(voltages, coefs, block_ids, tile_owner):
    chan_count = coefs.shape[1]
    parts = lax.axis_size("ft")
    fits = (
        voltages.shape[1] == chan_count
        and parts == SPECTRA
        and voltages.shape[2] == CHUNKS * LANES
        and chan_count == RADIX * LANES
        and (chan_count // RADIX) % AVG == 0
        and lax.axis_size("bl") == 4
    )
    if fits:
        return per_device_packed(voltages, coefs, block_ids, tile_owner)
    return per_device_general(voltages, coefs, block_ids, tile_owner)


def solution(mesh):
    return jax.shard_map(
        per_device,
        mesh=mesh,
        in_specs=(P(None, ("grp", "ft"), "bl"), P(), P(), P("grp")),
        out_specs=P(None, ("grp", "ft"), "bl", None, None),
        check_vma=False,
    )
```
